32 devices in a mesh: blk: 8 (over z, y), img: 4 (over x, core).
Axes of the slice: x: 2, y: 2, z: 4, core: 2. Of those that a mesh axis runs over, the one named last changes fastest.
Arguments:
- images: bfloat16 [4096, 1152], P(('blk', 'img')), may hold values from -0.1875 to 0.1875
- texts: bfloat16 [4096, 1152], P(('blk', 'img')), may hold values from -0.1875 to 0.1875
- cache: bfloat16 [4096, 1152], P(('blk', 'img')), may hold values from -0.1875 to 0.1875
- mate_owner: int32 [4096, 4], P(('blk', 'img')), may hold values from 0 to 31, all different within a row; in each aligned block of 128 rows (0 to 127, 128 to 255, ...) at most 32 rows name the same one
- mate_row: int32 [4096, 4], P(('blk', 'img')), may hold values from 0 to 127
- mate_count: int32 [4096], P(('blk', 'img')), may hold values from 1 to 4
- log_scale: float32 [1], replicated, may hold values from 1.8 to 2.6
- bias: float32 [1], replicated, may hold values from -6 to -2
Outputs:
- image_grad: float32 [4096, 1152], P(('blk', 'img'))
- text_grad: float32 [4096, 1152], P(('blk', 'img'))
- cache_grad: float32 [4096, 1152], P(('blk', 'img'))
The draws below stay inside these ranges and needn't reach their ends.
Inputs may be any that keep to these rules, and one draw needn't show every extreme that they name: `mate_owner`: among the 4 entries of the 128 rows of one device, each owner is named at most 32 times, and some device names some owner exactly 32 times; within a row the owners differ.
All inputs are finite; a program needn't handle non-finite values.
Results may differ from the reference program's by a relative error of at most 0.0034.
Values may be sent and summed in bfloat16 or wider, within the bound.
No kernel may reach another device: no remote copies, remote signals or barrier semaphores. Data moves between devices by JAX's collectives and lax.ppermute only.
A program may use at most 128 MiB of HBM per device.

```python
import math
import jax
import jax.numpy as jnp
import numpy as np
from jax import lax

D = 1152
IMG_DEV = 128
MATES = 4
CACHE_DEV = 128
PAIRS = 4096
OWNERS = 32
CACHE_ROWS = 4096
CAP = 32


def touch_ends(values, rng, smallest, top_value):
    longest = values.shape.index(max(values.shape))
    spots = []
    for shift in (0, 1):
        where = [jax.random.randint(jax.random.fold_in(rng, axis), (), 0, length) for axis, length in enumerate(values.shape)]
        where[longest] = (where[longest] + shift) % values.shape[longest]
        spots.append(tuple(where))
    return values.at[spots[0]].set(smallest).at[spots[1]].set(top_value)


def level_of(own_key, dims, shards, low, largest):
    def one(position, blocks):
        steps = jax.random.uniform(jax.random.fold_in(jax.random.fold_in(own_key, 6), position), (blocks,), jnp.float32, low / len(shards), largest / len(shards))
        return jnp.repeat(jnp.exp(steps), dims[position] // blocks).reshape((-1,) + (1,) * (len(dims) - position - 1))

    factor_of = one(*shards[0])
    for cut in shards[1:]:
        factor_of = factor_of * one(*cut)
    return factor_of


def deal_out(key, own, number, rows, amount, top, reach, slope):
    ranking = jax.random.permutation(key, amount)
    packed, usual = shares(amount, rows * top, reach, slope, True), shares(amount, rows * top, reach, slope, False)
    places = jnp.arange(amount)

    def named(sizes, rotation):
        used = int((sizes > 0).sum())
        fixed = max(1, used // 4)
        moved = fixed + (places - fixed + rotation * (used - fixed)) % max(1, amount - fixed)
        return jnp.zeros((amount,), jnp.int32).at[ranking[jnp.where(places < fixed, places, moved)]].set(jnp.asarray(sizes, jnp.int32))

    sizes = jnp.where(number % 4 == 0, named(packed, number // 4), named(usual, number - number // 4 - 1))
    mixed = jax.random.permutation(jax.random.fold_in(own, 3), amount)
    donor, receiver = mixed[0:amount // 2 * 2:2], mixed[1:amount // 2 * 2:2]
    room = jnp.minimum(sizes[donor] - 1, reach - sizes[receiver]) // 2
    room = jnp.where((donor == ranking[0]) | (receiver == ranking[0]) | (sizes[receiver] == 0), 0, jnp.maximum(room, 0))
    moved = jax.random.randint(jax.random.fold_in(own, 4), (amount // 2,), 0, 1 << 20) % (room + 1)
    sizes = sizes.at[donor].add(-moved).at[receiver].add(moved)
    labels = jnp.searchsorted(jnp.cumsum(sizes), jnp.arange(rows * top), side="right").astype(jnp.int32)
    listing = labels.reshape(top, rows).T
    listing = listing[jax.random.permutation(jax.random.fold_in(own, 1), rows)]
    rotation = jax.random.randint(jax.random.fold_in(own, 2), (rows, 1), 0, top)
    return jnp.take_along_axis(listing, (jnp.arange(top)[None, :] + rotation) % top, axis=1)


def shares(count, total, bound, skew, full):
    portions = [(1 << 20) // math.isqrt(grade ** skew) + 1 for grade in range(1, count + 1)]
    largest = bound if full else min(bound, max(-(-total // count), total * portions[0] // sum(portions)))
    least = 1 if total - largest >= count - 1 else 0
    holding, surplus = [largest] + [least] * (count - 1), total - largest - least * (count - 1)
    while surplus > 0:
        movable = [i for i in range(1, count) if holding[i] < largest] or [i for i in range(1, count) if holding[i] < bound]
        pool, left = sum([portions[i] for i in movable]), surplus
        for i in movable:
            addition = min(bound - holding[i], max(1, left * portions[i] // pool), surplus)
            holding[i] = holding[i] + addition
            surplus = surplus - addition
    return np.array(holding)


def scatter_about(stream_key, extent, deviation, reach, split=(), kind=jnp.bfloat16):
    loudness = level_of(stream_key, extent, split, -0.22, 0.18) if split else 1.0
    values = jax.random.normal(stream_key, extent, jnp.float32) * deviation * loudness
    return jnp.minimum(jnp.maximum(values, -reach), reach).astype(kind)


def setup_inputs(seed: int = 0) -> dict:
    arg_keys = jax.random.split(jax.random.key(seed), 9)
    images = scatter_about(arg_keys[0], (PAIRS, D), 0.03, 0.1875, ((0, 32),))
    texts = scatter_about(arg_keys[1], (PAIRS, D), 0.03, 0.1875, ((0, 32),))
    cache = scatter_about(arg_keys[2], (CACHE_ROWS, D), 0.03, 0.1875, ((0, 32),))
    mate_owner_keys = jax.random.split(jax.random.fold_in(arg_keys[3], 1), PAIRS // IMG_DEV)
    mate_owner_turns = jax.random.permutation(jax.random.fold_in(arg_keys[3], 3), PAIRS // IMG_DEV)
    mate_owner = jax.vmap(lambda own, number: deal_out(jax.random.fold_in(arg_keys[3], 2), own, number, IMG_DEV, OWNERS, MATES, CAP, 2))(mate_owner_keys, mate_owner_turns).reshape((PAIRS, MATES))
    mate_row = touch_ends(jax.random.randint(arg_keys[4], (PAIRS, MATES), 0, CACHE_DEV), jax.random.fold_in(arg_keys[4], 1), 0, CACHE_DEV - 1).astype(jnp.int32)
    mate_count = touch_ends(jax.random.randint(arg_keys[5], (PAIRS,), 1, MATES + 1), jax.random.fold_in(arg_keys[5], 1), 1, MATES).astype(jnp.int32)
    log_scale = jnp.clip(jax.random.uniform(arg_keys[6], (1,), jnp.float32, 1.8, 2.6), 1.8, 2.6)
    bias = jnp.clip(jax.random.uniform(arg_keys[7], (1,), jnp.float32, -6.0, -2.0), -6.0, -2.0)
    return dict(images=images, texts=texts, cache=cache, mate_owner=mate_owner, mate_row=mate_row, mate_count=mate_count, log_scale=log_scale, bias=bias)


def reference(images, texts, cache, mate_owner, mate_row, mate_count, log_scale, bias):
    scale = jnp.exp(log_scale[0])
    offset = bias[0]
    total_rows = images.shape[0]
    width = images.shape[1]
    block = min(512, total_rows)
    count = total_rows // block
    columns = jnp.arange(total_rows, dtype=jnp.int32)

    def step(tgrad, index):
        start = (index * block).astype(jnp.int32)
        rows_img = lax.dynamic_slice_in_dim(images, start, block, 0)
        logits = scale * jnp.dot(rows_img, texts.T, preferred_element_type=jnp.float32) + offset
        ids = start + jnp.arange(block, dtype=jnp.int32)
        same = (ids[:, None] == columns[None, :]).astype(jnp.float32)
        coeff = (scale * (jax.nn.sigmoid(logits) - same)).astype(jnp.bfloat16)
        igrad = jnp.dot(coeff, texts, preferred_element_type=jnp.float32)
        tgrad = tgrad + jnp.dot(coeff.T, rows_img, preferred_element_type=jnp.float32)
        return tgrad, igrad

    text_grad, image_parts = lax.scan(step, jnp.zeros((total_rows, width), jnp.float32), jnp.arange(count, dtype=jnp.int32))
    image_grad = image_parts.reshape(total_rows, width)
    ids = (mate_owner * CACHE_DEV + mate_row).astype(jnp.int32)
    mate_emb = cache[ids]
    mate_logit = scale * jnp.einsum("rd,rkd->rk", images.astype(jnp.float32), mate_emb.astype(jnp.float32)) + offset
    live = jnp.arange(MATES, dtype=jnp.int32)[None, :] < mate_count[:, None]
    mate_coeff = jnp.where(live, scale * (jax.nn.sigmoid(mate_logit) - 1.0), 0.0).astype(jnp.bfloat16)
    image_grad = image_grad + jnp.einsum("rk,rkd->rd", mate_coeff.astype(jnp.float32), mate_emb.astype(jnp.float32))
    terms = mate_coeff.astype(jnp.float32)[:, :, None] * images.astype(jnp.float32)[:, None, :]
    cache_grad = jnp.zeros((CACHE_ROWS, width), jnp.float32).at[ids.reshape(-1)].add(terms.reshape(-1, width))
    return image_grad, text_grad, cache_grad
```

```python
import jax
import jax.numpy as jnp
from jax import lax
from jax.sharding import Mesh, PartitionSpec as P

AXES = ("z", "y", "x", "c")
BF16 = jnp.bfloat16
F32 = jnp.float32


def dot(a, b, dims):
    return lax.dot_general(a, b, (dims, ((), ())), preferred_element_type=F32)


def shards(images, texts, cache, mate_owner, mate_row, mate_count, log_scale, bias):
    scale = jnp.exp(log_scale[0])
    offset = bias[0]
    rows, width = images.shape
    cache_rows = cache.shape[0]
    mates = mate_owner.shape[1]
    n_z = lax.axis_size("z")
    n_y = lax.axis_size("y")
    n_x = lax.axis_size("x")
    n_c = lax.axis_size("c")
    z, y, x, c = (lax.axis_index(a) for a in AXES)

    def send(value, kz=0, ky=0, kx=0, kc=0):
        pairs = []
        for d in range(n_z * n_y * n_x * n_c):
            rest, dc = divmod(d, n_c)
            rest, dx = divmod(rest, n_x)
            dz, dy = divmod(rest, n_y)
            peer = (((dz ^ kz) * n_y + (dy ^ ky)) * n_x + (dx ^ kx)) * n_c + (dc ^ kc)
            pairs.append((d, peer))
        return lax.ppermute(value, AXES, pairs)

    live = jnp.arange(mates, dtype=jnp.int32)[None, :] < mate_count[:, None]
    owner = jnp.where(live, mate_owner, -1)
    ids = jnp.concatenate([owner.T, mate_row.T], axis=0).astype(BF16)
    ids = jnp.pad(ids, ((0, 0), (0, width - rows)))
    packet = jnp.concatenate([images, ids], axis=0)

    far = [k for k in range(n_z - 1, 0, -1)]
    sides = [(j // n_x, j % n_x) for j in range(n_y * n_x)]
    packets = {}
    packets[0] = packet
    for k in far:
        packets[k] = send(packet, kz=k)
    text_parts = [texts] + [send(texts, ky=a, kx=b) for a, b in sides[1:]]
    cache_parts = [cache] + [send(cache, ky=a, kx=b) for a, b in sides[1:]]
    text_all = jnp.concatenate(text_parts, axis=0)
    cache_all = jnp.concatenate(cache_parts, axis=0)

    def place(a, b):
        return ((z * n_y + (y ^ a)) * n_x + (x ^ b)) * n_c + c

    row = jnp.arange(cache_rows, dtype=jnp.int32)
    cache_ids = jnp.concatenate([place(a, b) * cache_rows + row for a, b in sides]).astype(F32)

    def group(k):
        mine = packets[k]
        other = send(mine, kc=1)
        left = jnp.concatenate([mine[:rows], other[:rows]], axis=0)
        tags = jnp.concatenate([mine[rows:, :rows], other[rows:, :rows]], axis=1).astype(F32)
        tags = jnp.where(tags[:mates] < 0, -1.0, tags[:mates] * cache_rows + tags[mates:])
        return left, tags

    def text_coeff(left, k):
        value = jax.nn.sigmoid(scale * dot(text_all, left, ((1,), (1,))) + offset)
        if k == 0:
            i = lax.broadcasted_iota(jnp.int32, value.shape, 0)
            j = lax.broadcasted_iota(jnp.int32, value.shape, 1)
            value = value - ((i == j) & (i < rows)).astype(F32)
        return (scale * value).astype(BF16)

    def cache_coeff(left, tags):
        value = jax.nn.sigmoid(scale * dot(cache_all, left, ((1,), (1,))) + offset) - 1.0
        hit = cache_ids[:, None] == tags[0][None, :]
        for m in range(1, mates):
            hit = hit | (cache_ids[:, None] == tags[m][None, :])
        return jnp.where(hit, scale * value, 0.0).astype(BF16)

    order = [0] + far
    lefts, t_coeffs, c_coeffs, sums = [], [], [], {}
    for k in order:
        left, tags = group(k)
        tc = text_coeff(left, k)
        cc = cache_coeff(left, tags)
        part = dot(tc, text_all, ((0,), (0,))) + dot(cc, cache_all, ((0,), (0,)))
        given = send(part[rows:].astype(BF16), kc=1)
        total = part[:rows] + given.astype(F32)
        if k:
            total = send(total.astype(BF16), kz=k).astype(F32)
        sums[k] = total
        lefts.append(left)
        t_coeffs.append(tc)
        c_coeffs.append(cc)
    left_all = jnp.concatenate(lefts, axis=0)
    t_all = jnp.concatenate(t_coeffs, axis=1)
    c_all = jnp.concatenate(c_coeffs, axis=1)

    def column_grad(coeff, size):
        own = dot(coeff[:size], left_all, ((1,), (0,)))
        away = dot(coeff[size:], left_all, ((1,), (0,))).astype(BF16)
        for j in range(len(sides) - 1, 0, -1):
            a, b = sides[j]
            own = own + send(away[(j - 1) * size : j * size], ky=a, kx=b).astype(F32)
        return own

    text_grad = column_grad(t_all, rows)
    cache_grad = column_grad(c_all, cache_rows)
    image_grad = sums[0]
    for k in far:
        image_grad = image_grad + sums[k]
    return image_grad, text_grad, cache_grad


def solution(mesh):
    n_blk, n_img = mesh.devices.shape
    grid = Mesh(mesh.devices.reshape(n_blk // 2, 2, n_img // 2, 2), AXES)
    split = P(AXES, None)
    return jax.shard_map(
        shards,
        mesh=grid,
        in_specs=(split, split, split, split, split, P(AXES), P(), P()),
        out_specs=(split, split, split),
        check_vma=False,
    )
```

```python
import functools

import jax
import jax.numpy as jnp
from jax import lax
from jax.experimental import pallas as pl
from jax.experimental.pallas import tpu as pltpu
from jax.sharding import Mesh, PartitionSpec as P

AXES = ("z", "y", "x", "c")
BF16 = jnp.bfloat16
F32 = jnp.float32
VMEM = pl.BlockSpec(memory_space=pltpu.VMEM)
SMEM = pl.BlockSpec(memory_space=pltpu.SMEM)
PARAMS = pltpu.CompilerParams(vmem_limit_bytes=40 << 20)


def dot(a, b, dims):
    return lax.dot_general(a, b, (dims, ((), ())), preferred_element_type=F32)


def stack(refs):
    return jnp.concatenate([r[...] for r in refs], axis=0)


def cost(flops, count, moved):
    return pl.CostEstimate(flops=flops, bytes_accessed=moved, transcendentals=count)


def text_kernel(first, n_parts, num_ref, *refs):
    texts, left, out = refs[:n_parts], refs[n_parts:-1], refs[-1]
    value = jax.nn.sigmoid(num_ref[0] * dot(stack(texts), stack(left), ((1,), (1,))) + num_ref[1])
    if first:
        rows = left[0].shape[0]
        i = lax.broadcasted_iota(jnp.int32, value.shape, 0)
        j = lax.broadcasted_iota(jnp.int32, value.shape, 1)
        value = value - ((i == j) & (i < rows)).astype(F32)
    out[...] = (num_ref[0] * value).astype(BF16)


def cache_kernel(n_parts, mates, num_ref, *refs):
    texts, caches = refs[:n_parts], refs[n_parts : 2 * n_parts]
    left = refs[2 * n_parts : -5]
    tag_ref, coeff_ref, out_ref, keep_ref, give_ref = refs[-5:]
    size = caches[0].shape[0]
    rows = left[0].shape[0]
    all_cache = stack(caches)
    value = jax.nn.sigmoid(num_ref[0] * dot(all_cache, stack(left), ((1,), (1,))) + num_ref[1])
    value = num_ref[0] * (value - 1.0)
    tags = tag_ref[...]
    index = lax.broadcasted_iota(jnp.int32, (size, tags.shape[1]), 0).astype(F32)
    for j in range(n_parts):
        near = tags - num_ref[2 + j]
        hit = index == near[0:1]
        for m in range(1, mates):
            hit = hit | (index == near[m : m + 1])
        block = slice(j * size, (j + 1) * size)
        out_ref[block, :] = jnp.where(hit, value[block], 0.0).astype(BF16)
    part = dot(coeff_ref[...], stack(texts), ((0,), (0,)))
    part = part + dot(out_ref[...], all_cache, ((0,), (0,)))
    keep_ref[...] = part[:rows]
    give_ref[...] = part[rows:].astype(BF16)


def column_kernel(n_groups, *refs):
    coeffs, left, outs = refs[:n_groups], refs[n_groups : 3 * n_groups], refs[3 * n_groups :]
    every = jnp.concatenate([r[...] for r in coeffs], axis=1)
    result = dot(every, stack(left), ((1,), (0,)))
    size = outs[0].shape[0]
    for j, out in enumerate(outs):
        out[...] = result[j * size : (j + 1) * size].astype(out.dtype)


def shards(images, texts, cache, mate_owner, mate_row, mate_count, log_scale, bias):
    rows, width = images.shape
    cache_rows = cache.shape[0]
    mates = mate_owner.shape[1]
    n_z, n_y, n_x, n_c = (lax.axis_size(a) for a in AXES)
    z, y, x, c = (lax.axis_index(a) for a in AXES)
    parts = n_y * n_x

    def send(value, kz=0, ky=0, kx=0, kc=0):
        pairs = []
        for d in range(n_z * n_y * n_x * n_c):
            rest, dc = divmod(d, n_c)
            rest, dx = divmod(rest, n_x)
            dz, dy = divmod(rest, n_y)
            peer = (((dz ^ kz) * n_y + (dy ^ ky)) * n_x + (dx ^ kx)) * n_c + (dc ^ kc)
            pairs.append((d, peer))
        return lax.ppermute(value, AXES, pairs)

    far = [k for k in range(n_z - 1, 0, -1)]
    order = [0] + far

    mine = {0: images}
    for k in far:
        mine[k] = send(images, kz=k)
    left = {k: (mine[k], send(mine[k], kc=1)) for k in order}

    text_x = send(texts, kx=1)
    cache_y = send(cache, ky=1)
    cache_x = send(cache, kx=1)
    text_y = send(texts, ky=1)
    text_parts = [texts, text_x, text_y, send(text_x, ky=1)]
    cache_parts = [cache, cache_x, cache_y, send(cache_y, kx=1)]
    place = [((z * n_y + (y ^ (j // n_x))) * n_x + (x ^ (j % n_x))) * n_c + c for j in range(parts)]

    live = jnp.arange(mates, dtype=jnp.int32)[None, :] < mate_count[:, None]
    tags = jnp.stack([jnp.where(live, mate_owner, -1).T, mate_row.T]).astype(BF16)[None]
    tags = jnp.concatenate([tags, send(tags, kc=1)], axis=0)
    step = 1
    while step < n_z:
        tags = jnp.concatenate([tags, send(tags, kz=step)], axis=0)
        step *= 2
    tags = tags.astype(F32)
    tags = jnp.where(tags[:, 0] < 0, -1.0, tags[:, 0] * cache_rows + tags[:, 1])
    tags = tags.reshape(n_z, n_c, mates, rows).swapaxes(1, 2).reshape(n_z, mates, n_c * rows)

    numbers = [jnp.exp(log_scale[0]), bias[0]] + [(p * cache_rows).astype(F32) for p in place]
    numbers = jnp.stack(numbers)

    group = n_c * rows
    total = parts * rows
    t_coeff, c_coeff, sums = {}, {}, {}
    for k in order:
        t_coeff[k] = pl.pallas_call(
            functools.partial(text_kernel, k == 0, parts),
            out_shape=jax.ShapeDtypeStruct((total, group), BF16),
            in_specs=[SMEM] + [VMEM] * (parts + n_c),
            out_specs=VMEM,
            compiler_params=PARAMS,
            cost_estimate=cost(2 * total * group * width, total * group, 2 * width * total),
            name="text_coeff",
        )(numbers, *text_parts, *left[k])
        c_coeff[k], keep, give = pl.pallas_call(
            functools.partial(cache_kernel, parts, mates),
            out_shape=(
                jax.ShapeDtypeStruct((parts * cache_rows, group), BF16),
                jax.ShapeDtypeStruct((rows, width), F32),
                jax.ShapeDtypeStruct((rows, width), BF16),
            ),
            in_specs=[SMEM] + [VMEM] * (2 * parts + n_c + 2),
            out_specs=(VMEM,) * 3,
            compiler_params=PARAMS,
            cost_estimate=cost(6 * total * group * width, total * group, 4 * width * total),
            name="cache_coeff",
        )(numbers, *text_parts, *cache_parts, *left[k], tags[k], t_coeff[k])
        value = keep + send(give, kc=1).astype(F32)
        if k:
            value = send(value.astype(BF16), kz=k).astype(F32)
        sums[k] = value

    every_left = [p for k in order for p in left[k]]

    def column(coeff, size, kinds, name):
        return pl.pallas_call(
            functools.partial(column_kernel, n_z),
            out_shape=tuple(jax.ShapeDtypeStruct((size, width), d) for d in kinds),
            in_specs=[VMEM] * (3 * n_z),
            out_specs=(VMEM,) * parts,
            compiler_params=PARAMS,
            cost_estimate=cost(2 * total * group * n_z * width, 0, 2 * width * n_z * group),
            name=name,
        )(*[coeff[k] for k in order], *every_left)

    own, to_x, to_y, to_far = column(t_coeff, rows, (F32, BF16, F32, BF16), "text_grad")
    passed = (to_y + send(to_far, kx=1).astype(F32)).astype(BF16)
    text_grad = own + send(to_x, kx=1).astype(F32) + send(passed, ky=1).astype(F32)
    own, to_x, to_y, to_far = column(c_coeff, cache_rows, (F32, F32, BF16, BF16), "cache_grad")
    passed = (to_x + send(to_far, ky=1).astype(F32)).astype(BF16)
    cache_grad = own + send(to_y, ky=1).astype(F32) + send(passed, kx=1).astype(F32)
    image_grad = sums[0]
    for k in far:
        image_grad = image_grad + sums[k]
    return image_grad, text_grad, cache_grad


def solution(mesh):
    n_blk, n_img = mesh.devices.shape
    grid = Mesh(mesh.devices.reshape(n_blk // 2, 2, n_img // 2, 2), AXES)
    split = P(AXES, None)
    return jax.shard_map(
        shards,
        mesh=grid,
        in_specs=(split, split, split, split, split, P(AXES), P(), P()),
        out_specs=(split, split, split),
        check_vma=False,
    )
```
